256 devices in a mesh: cls: 8 (over z), dom: 32 (over x, y, core).
Axes of the slice: x: 4, y: 4, z: 8, core: 2. Of those that a mesh axis runs over, the one named last changes fastest.
Arguments:
- particles: bfloat16 [32768, 8192], P(('cls', 'dom')), may hold values from -6 to 6
- assign: int32 [32768, 1], P(('cls', 'dom')), may hold values from 0 to 15; in each aligned block of 128 rows (0 to 127, 128 to 255, ...) at most 16 rows name the same one
- inv_sigma: bfloat16 [32768], P(('cls', 'dom')), may hold values from 0.5 to 300, as said below
- projections: bfloat16 [16, 64, 8192], P('cls', 'dom'), may hold values from -0.0625 to 0.0625
Outputs:
- class_sums: float32 [16, 64, 8192], P('cls', 'dom')
- evidence: float32 [32768], P(('cls', 'dom'))
The draws below stay inside these ranges and needn't reach their ends.
Inputs may be any that keep to these rules, and one draw needn't show every extreme that they name: `assign`: among the 128 particles of one device (aligned blocks of rows) no class is named more than 16 times, a bound that some block reaches. `inv_sigma`: each particle's noise precision, positive.
All inputs are finite; a program needn't handle non-finite values.
Results may differ from the reference program's by a relative error of at most 0.0023.
Values may be sent and summed in bfloat16 or wider, within the bound.
A program may use at most 64 MiB of HBM per device.

```python
import math
import jax
import jax.numpy as jnp
import numpy as np
from jax import lax

F = 8192
PART_DEV = 128
K = 16
R = 64
CAP = 16
PARTICLES = 32768
N_CLS = 8
N_DOM = 32


def draw_inv_sigma(key, part):
    lower, upper = (0.5, 16.0)
    fraction = jax.random.uniform(key, (PARTICLES,), jnp.float32)
    values = jnp.exp(math.log(lower) + fraction * (math.log(upper) - math.log(lower)))
    return values.astype(jnp.bfloat16)


def steps_of(stream_key, shape, split, smallest, high):
    level = 1.0
    for position, parts in split:
        draws = jax.random.uniform(jax.random.fold_in(jax.random.fold_in(stream_key, 6), position), (parts,), jnp.float32, smallest / len(split), high / len(split))
        level = level * jnp.repeat(jnp.exp(draws), shape[position] // parts).reshape((-1,) + (1,) * (len(shape) - 1 - position))
    return level


def assign_block(key, own, number, rows, number_of, top, limit, slope):
    ranking = jax.random.permutation(key, number_of)
    crowded, ordinary = load_shares(number_of, rows * top, limit, slope, True), load_shares(number_of, rows * top, limit, slope, False)
    places = jnp.arange(number_of)

    def named(sizes, turn):
        used = int((sizes > 0).sum())
        fixed = max(1, used // 4)
        moved = fixed + (places - fixed + turn * (used - fixed)) % max(1, number_of - fixed)
        return jnp.zeros((number_of,), jnp.int32).at[ranking[jnp.where(places < fixed, places, moved)]].set(jnp.asarray(sizes, jnp.int32))

    sizes = jnp.where(number % 4 == 0, named(crowded, number // 4), named(ordinary, number - number // 4 - 1))
    mixed = jax.random.permutation(jax.random.fold_in(own, 3), number_of)
    giver, receiver = mixed[0:number_of // 2 * 2:2], mixed[1:number_of // 2 * 2:2]
    margin = jnp.minimum(sizes[giver] - 1, limit - sizes[receiver]) // 2
    margin = jnp.where((giver == ranking[0]) | (receiver == ranking[0]) | (sizes[receiver] == 0), 0, jnp.maximum(margin, 0))
    moved = jax.random.randint(jax.random.fold_in(own, 4), (number_of // 2,), 0, 1 << 20) % (margin + 1)
    sizes = sizes.at[giver].add(-moved).at[receiver].add(moved)
    labels = jnp.searchsorted(jnp.cumsum(sizes), jnp.arange(rows * top), side="right").astype(jnp.int32)
    listing = labels.reshape(top, rows).T
    listing = listing[jax.random.permutation(jax.random.fold_in(own, 1), rows)]
    turn = jax.random.randint(jax.random.fold_in(own, 2), (rows, 1), 0, top)
    return jnp.take_along_axis(listing, (jnp.arange(top)[None, :] + turn) % top, axis=1)


def load_shares(amount, total, limit, lean, full):
    loads = [(1 << 20) // math.isqrt(rank ** lean) + 1 for rank in range(1, amount + 1)]
    largest = limit if full else min(limit, max(-(-total // amount), total * loads[0] // sum(loads)))
    least = 1 if total - largest >= amount - 1 else 0
    holding, surplus = [largest] + [least] * (amount - 1), total - largest - least * (amount - 1)
    while surplus > 0:
        candidates = [i for i in range(1, amount) if holding[i] < largest] or [i for i in range(1, amount) if holding[i] < limit]
        mass, left = sum([loads[i] for i in candidates]), surplus
        for i in candidates:
            extra = min(limit - holding[i], max(1, left * loads[i] // mass), surplus)
            holding[i] = holding[i] + extra
            surplus = surplus - extra
    return np.array(holding)


def bell_draw(stream_key, dims, scale, bound, shards=(), kind=jnp.bfloat16):
    level = steps_of(stream_key, dims, shards, -0.22, 0.18) if shards else 1.0
    values = jax.random.normal(stream_key, dims, jnp.float32) * scale * level
    return jnp.minimum(jnp.maximum(values, -bound), bound).astype(kind)


def setup_inputs(seed: int = 0) -> dict:
    keys = jax.random.split(jax.random.key(seed), 5)
    particles = bell_draw(keys[0], (PARTICLES, F), 1.0, 6.0, ((0, 256),))
    assign_keys = jax.random.split(jax.random.fold_in(keys[1], 1), PARTICLES // PART_DEV)
    assign_turns = jax.random.permutation(jax.random.fold_in(keys[1], 3), PARTICLES // PART_DEV)
    assign = jax.vmap(lambda own, number: assign_block(jax.random.fold_in(keys[1], 2), own, number, PART_DEV, K, 1, CAP, 1))(assign_keys, assign_turns).reshape((PARTICLES, 1))
    inv_sigma = draw_inv_sigma(jax.random.fold_in(keys[4], 71), 0)
    projections = bell_draw(keys[3], (K, R, F), F ** -0.5, 0.0625, ((0, 8), (1, 32)))
    return {"particles": particles, "assign": assign, "inv_sigma": inv_sigma, "projections": projections}


def reference(particles, assign, inv_sigma, projections):
    classes = projections.shape[0]
    most_rows = N_CLS * N_DOM * CAP
    total = particles.shape[0]
    class_id = assign[:, 0]
    halves = 0.5 * jnp.sum(jnp.square(projections.astype(jnp.float32)), axis=2)

    def single(klass):
        index_list = jnp.nonzero(class_id == klass, size=most_rows, fill_value=total)[0].astype(jnp.int32)
        is_live = index_list < total
        safe_index = jnp.minimum(index_list, total - 1)
        picked = particles[safe_index]
        precision = jnp.where(is_live, inv_sigma[safe_index].astype(jnp.float32), 0.0)
        project = lax.dynamic_index_in_dim(projections, klass, 0, keepdims=False)
        class_half = lax.dynamic_index_in_dim(halves, klass, 0, keepdims=False)
        products = jnp.dot(picked, project.T, preferred_element_type=jnp.float32)
        scores = precision[:, None] * (products - class_half[None, :])
        largest = jnp.max(scores, axis=1, keepdims=True)
        exponent = jnp.exp(scores - largest)
        totals = jnp.sum(exponent, axis=1, keepdims=True)
        weights = jnp.where(is_live[:, None], exponent / totals, 0.0).astype(jnp.bfloat16)
        sums = lax.dot_general(weights, picked, (((0,), (0,)), ((), ())), preferred_element_type=jnp.float32)
        log_total = largest[:, 0] + jnp.log(totals[:, 0])
        return sums, log_total, index_list

    sums, log_total, index_list = lax.map(single, jnp.arange(classes, dtype=jnp.int32))
    evidence = jnp.zeros((total,), jnp.float32).at[index_list.reshape(-1)].set(log_total.reshape(-1), mode="drop")
    return sums, evidence
```

```python
import functools

import jax
import jax.numpy as jnp
from jax import lax
from jax.experimental import pallas as pl
from jax.experimental.pallas import tpu as pltpu
from jax.sharding import PartitionSpec as P

MESH = pl.DeviceIdType.MESH
TWIST = True
NX, NY, NZ = 4, 4, 8
F32 = jnp.float32
BF16 = jnp.bfloat16


def _mod(v, n):
    return lax.rem(v + 2 * n, n)


def _device(x, y, z, c):
    return (_mod(z, NZ), (_mod(x, NX) * NY + _mod(y, NY)) * 2 + c)


def _shift(k):
    i, j = lax.div(k, 4), lax.rem(k, 4)
    if not TWIST:
        return i, j, 0
    low_i, low_j = jnp.where(i == 3, -1, i), jnp.where(j == 3, -1, j)
    both = jnp.where(jnp.minimum(low_i, low_j) > 0, jnp.minimum(low_i, low_j), -1)
    flat = (low_i == 0) | (low_j == 0) | (low_i + low_j == 0)
    dz = jnp.where(flat, 0, both)
    return i - dz, j - dz, dz


def kernel(
    x_ref, a_ref, s_ref, j_ref, out_ref, ev_ref,
    X, A, J1, ASM, PJ, H, T, SS, SR, WS, WB, WM, ACC, RS, RR, FS,
    lsem, xs, xr, as_, ar, js, jr, gs, gr, ss, sr, ws, wr, rs, rr, fs, fr,
):
    d, z = lax.axis_index("dom"), lax.axis_index("cls")
    c = lax.rem(d, 2)
    y = lax.rem(lax.div(d, 2), NY)
    x = lax.div(d, 2 * NY)
    t = z if TWIST else 0

    def colour(i, j, core):
        return (_mod(x + t + i, NX) * NY + _mod(y + t + j, NY)) * 2 + core

    def cols(s):
        return pl.ds(pl.multiple_of(s * 256, 256), 256)

    def peer(k, core, sign=1):
        dx, dy, dz = _shift(k)
        return _device(x + sign * dx, y + sign * dy, z + sign * dz, core)

    def plane_peer(k, core):
        return _device(x + lax.div(k, 4), y + lax.rem(k, 4), z, core)

    def column_peer(h):
        if TWIST:
            return _device(x - h + 8, y - h + 8, z + h, c)
        return _device(x, y, z + h, c)

    def each(fn):
        fn(0, 1 - c)

        def body(k, _):
            fn(k, 0)
            fn(k, 1)
            return 0

        lax.fori_loop(1, 16, body, 0)

    barrier = pltpu.get_barrier_semaphore()

    def greet(device):
        pl.semaphore_signal(barrier, inc=1, device_id=device, device_id_type=MESH)

    each(lambda k, core: greet(plane_peer(k, core)))
    for h in range(1, NZ):
        greet(column_peer(h))
    greeted = 31 + 7
    if TWIST:
        for dx, dy, dz in ((0, 0, 1), (1, 0, 1), (0, 1, 1), (0, 0, 2)):
            for sign in (1, -1):
                for core in (0, 1):
                    greet(_device(x + sign * dx, y + sign * dy, z + sign * dz, core))
                    greeted += 1
    pl.semaphore_wait(barrier, greeted)

    def send_j(k, core):
        s = colour(lax.div(k, 4), lax.rem(k, 4), core)
        return pltpu.make_async_remote_copy(
            src_ref=j_ref.at[:, :, cols(s)], dst_ref=J1.at[d],
            send_sem=js.at[2 * k + core], recv_sem=jr.at[d],
            device_id=plane_peer(k, core), device_id_type=MESH)

    def recv_j(q):
        return pltpu.make_async_remote_copy(
            src_ref=J1.at[q], dst_ref=J1.at[q], send_sem=js.at[q], recv_sem=jr.at[q],
            device_id=plane_peer(1, c), device_id_type=MESH)

    def send_x(k, core):
        s = colour(lax.div(k, 4), lax.rem(k, 4), core)
        return pltpu.make_async_remote_copy(
            src_ref=x_ref.at[:, cols(s)], dst_ref=X.at[2 * k + c],
            send_sem=xs.at[2 * k + core], recv_sem=xr.at[2 * k + c],
            device_id=peer(k, core), device_id_type=MESH)

    def send_a(k, core):
        return pltpu.make_async_remote_copy(
            src_ref=a_ref, dst_ref=A.at[2 * k + c],
            send_sem=as_.at[2 * k + core], recv_sem=ar.at[2 * k + c],
            device_id=peer(k, core), device_id_type=MESH)

    def recv(buf, ssem, rsem, slot):
        return pltpu.make_async_remote_copy(
            src_ref=buf.at[slot], dst_ref=buf.at[slot], send_sem=ssem.at[slot], recv_sem=rsem.at[slot],
            device_id=peer(1, c), device_id_type=MESH)

    def send_s(k, core):
        return pltpu.make_async_remote_copy(
            src_ref=SS.at[2 * k + core], dst_ref=SR.at[2 * k + c],
            send_sem=ss.at[2 * k + core], recv_sem=sr.at[2 * k + c],
            device_id=peer(k, core, -1), device_id_type=MESH)

    def send_w(k, core):
        return pltpu.make_async_remote_copy(
            src_ref=WS, dst_ref=WB.at[2 * k + c],
            send_sem=ws.at[2 * k + core], recv_sem=wr.at[2 * k + c],
            device_id=peer(k, core), device_id_type=MESH)

    def send_g(h):
        return pltpu.make_async_remote_copy(
            src_ref=PJ.at[z], dst_ref=PJ.at[z], send_sem=gs.at[h], recv_sem=gr.at[z],
            device_id=column_peer(h), device_id_type=MESH)

    def recv_g(p):
        return pltpu.make_async_remote_copy(
            src_ref=PJ.at[p], dst_ref=PJ.at[p], send_sem=gs.at[p], recv_sem=gr.at[p],
            device_id=column_peer(1), device_id_type=MESH)

    def send_r(h):
        return pltpu.make_async_remote_copy(
            src_ref=RS.at[h], dst_ref=RR.at[h], send_sem=rs.at[h], recv_sem=rr.at[h],
            device_id=column_peer(h), device_id_type=MESH)

    def send_f(k, core):
        q = (_mod(x + lax.div(k, 4), NX) * NY + _mod(y + lax.rem(k, 4), NY)) * 2 + core
        return pltpu.make_async_remote_copy(
            src_ref=FS.at[q], dst_ref=out_ref.at[:, :, cols(colour(0, 0, c))],
            send_sem=fs.at[2 * k + core], recv_sem=fr.at[2 * k + c],
            device_id=plane_peer(k, core), device_id_type=MESH)

    def recv_f(k, core):
        return pltpu.make_async_remote_copy(
            src_ref=FS.at[0], dst_ref=out_ref.at[:, :, cols(colour(-lax.div(k, 4), -lax.rem(k, 4), core))],
            send_sem=fs.at[2 * k + core], recv_sem=fr.at[2 * k + core],
            device_id=plane_peer(k, core), device_id_type=MESH)

    mine = colour(0, 0, c)
    own_x = pltpu.make_async_copy(x_ref.at[:, cols(mine)], X.at[c], lsem.at[0])
    own_j = pltpu.make_async_copy(j_ref.at[:, :, cols(mine)], J1.at[d], lsem.at[1])
    own_j.start()
    each(lambda k, core: send_j(k, core).start())
    each(lambda k, core: send_a(k, core).start())
    own_x.start()
    each(lambda k, core: send_x(k, core).start())
    A[c] = a_ref[...]

    own_j.wait()
    def wait_j(q, _):
        @pl.when(q != d)
        def _():
            recv_j(q).wait_recv()
        return 0
    lax.fori_loop(0, 32, wait_j, 0)
    for q in range(32):
        for kk in range(2):
            ASM[kk * 64 + 2 * q : kk * 64 + 2 * q + 2, :] = J1[q, kk].astype(F32)
    PJ[z] = ASM[...].astype(BF16)
    for h in range(1, NZ):
        send_g(h).start()

    def wait_g(p, _):
        @pl.when(p != z)
        def _():
            recv_g(p).wait_recv()
        v = PJ[p].astype(F32)
        half = 0.5 * jnp.sum(v * v, axis=1, keepdims=True)
        H[p] = jnp.broadcast_to(half, (128, 128))
        return 0
    lax.fori_loop(0, NZ, wait_g, 0)

    own_x.wait()

    def wait_slot(k, core, buf, ssem, rsem):
        @pl.when((k != 0) | (c != core))
        def _():
            recv(buf, ssem, rsem, 2 * k + core).wait_recv()

    def score(k, _):
        for core in range(2):
            wait_slot(k, core, X, xs, xr)
            wait_slot(k, core, A, as_, ar)
        rows = X[pl.ds(2 * k, 2)].reshape(256, 256)
        T[...] = lax.dot_general(
            PJ[...].reshape(1024, 256), rows, (((1,), (1,)), ((), ())), preferred_element_type=F32)
        for core in range(2):
            ids = jnp.broadcast_to(A[2 * k + core], (64, 128))
            total = jnp.zeros((64, 128), F32)
            for m in range(16):
                part = T[m * 64 : (m + 1) * 64, core * 128 : (core + 1) * 128]
                half = H[m // 2, (m % 2) * 64 : (m % 2) * 64 + 64, :]
                total = jnp.where(ids == m, part - half, total)
            SS[2 * k + core] = total
        for core in range(2):
            @pl.when((k != 0) | (c != core))
            def _():
                send_s(k, core).start()
        return 0
    lax.fori_loop(0, 16, score, 0)

    def gather(k, total):
        for core in range(2):
            recv(SR, ss, sr, 2 * k + core).wait_recv()
            total = total + SR[2 * k + core]
        return total
    recv(SR, ss, sr, 1 - c).wait_recv()
    total = lax.fori_loop(1, 16, gather, SS[c] + SR[1 - c])
    scores = total * s_ref[...].astype(F32)
    largest = jnp.max(scores, axis=0, keepdims=True)
    expo = jnp.exp(scores - largest)
    sums = jnp.sum(expo, axis=0, keepdims=True)
    weight = (expo / sums).astype(BF16)
    WS[...] = weight
    WB[c] = weight
    each(lambda k, core: send_w(k, core).start())
    ev_ref[...] = largest + jnp.log(sums)

    ACC[...] = jnp.zeros_like(ACC)

    def accumulate(k, _):
        for core in range(2):
            wait_slot(k, core, WB, ws, wr)
        for core in range(2):
            ids = jnp.broadcast_to(A[2 * k + core], (64, 128))
            w = WB[2 * k + core].astype(F32)
            for m in range(16):
                WM[m * 64 : (m + 1) * 64, core * 128 : (core + 1) * 128] = jnp.where(ids == m, w, 0.0).astype(BF16)
        rows = X[pl.ds(2 * k, 2)].reshape(256, 256)
        ACC[...] += jnp.dot(WM[...], rows, preferred_element_type=F32)
        return 0
    lax.fori_loop(0, 16, accumulate, 0)

    for h in range(1, NZ):
        p = _mod(z + h, NZ)
        RS[h] = ACC[pl.ds(pl.multiple_of(p * 128, 128), 128), :].astype(BF16)
        send_r(h).start()
    final = ACC[pl.ds(pl.multiple_of(z * 128, 128), 128), :]
    for h in range(1, NZ):
        send_r(h).wait_recv()
        final = final + RR[h].astype(F32)
    ASM[...] = final
    for q in range(32):
        for kk in range(2):
            FS[q, kk] = ASM[kk * 64 + 2 * q : kk * 64 + 2 * q + 2, :]
    each(lambda k, core: send_f(k, core).start())
    out_ref[:, :, cols(mine)] = FS[d]
    each(lambda k, core: recv_f(k, core).wait_recv())

    for send in (send_j, send_a, send_x, send_s, send_w, send_f):
        each(lambda k, core, send=send: send(k, core).wait_send())
    for h in range(1, NZ):
        send_g(h).wait_send()
        send_r(h).wait_send()


def on_device(particles, assign, inv_sigma, projections):
    dma = pltpu.SemaphoreType.DMA
    vmem = pltpu.VMEM
    sums, evidence = pl.pallas_call(
        kernel,
        name="estep",
        out_shape=(
            jax.ShapeDtypeStruct((2, 2, 8192), F32),
            jax.ShapeDtypeStruct((1, 128), F32),
        ),
        in_specs=[
            pl.BlockSpec(memory_space=pl.ANY),
            pl.BlockSpec(memory_space=pltpu.VMEM),
            pl.BlockSpec(memory_space=pltpu.VMEM),
            pl.BlockSpec(memory_space=pl.ANY),
        ],
        out_specs=(
            pl.BlockSpec(memory_space=pltpu.VMEM),
            pl.BlockSpec(memory_space=pltpu.VMEM),
        ),
        scratch_shapes=[
            vmem((32, 128, 256), BF16),
            vmem((32, 1, 128), jnp.int32),
            vmem((32, 2, 2, 256), BF16),
            vmem((128, 256), F32),
            vmem((8, 128, 256), BF16),
            vmem((8, 128, 128), F32),
            vmem((1024, 256), F32),
            vmem((32, 64, 128), F32),
            vmem((32, 64, 128), F32),
            vmem((64, 128), BF16),
            vmem((32, 64, 128), BF16),
            vmem((1024, 256), BF16),
            vmem((1024, 256), F32),
            vmem((8, 128, 256), BF16),
            vmem((8, 128, 256), BF16),
            vmem((32, 2, 2, 256), F32),
            dma((2,)),
            dma((32,)), dma((32,)),
            dma((32,)), dma((32,)),
            dma((32,)), dma((32,)),
            dma((8,)), dma((8,)),
            dma((32,)), dma((32,)),
            dma((32,)), dma((32,)),
            dma((8,)), dma((8,)),
            dma((32,)), dma((32,)),
        ],
        compiler_params=pltpu.CompilerParams(collective_id=0, has_side_effects=True),
    )(particles, assign.reshape(1, 128), inv_sigma.reshape(1, 128), projections)
    return sums, evidence.reshape(128)


def solution(mesh):
    return jax.shard_map(
        on_device,
        mesh=mesh,
        in_specs=(
            P(("cls", "dom"), None),
            P(("cls", "dom"), None),
            P(("cls", "dom")),
            P("cls", "dom", None),
        ),
        out_specs=(P("cls", "dom", None), P(("cls", "dom"))),
        check_vma=False,
    )
```

```python
import functools

import jax
import jax.numpy as jnp
from jax import lax
from jax.experimental import pallas as pl
from jax.experimental.pallas import tpu as pltpu
from jax.sharding import PartitionSpec as P

MESH = pl.DeviceIdType.MESH
TWIST = True
EARLY = 7
ORDER = (2, 6, 3, 5, 4, 1, 7)
NX, NY, NZ = 4, 4, 8
F32 = jnp.float32
BF16 = jnp.bfloat16


def _mod(v, n):
    return v % n if isinstance(v, int) else v & (n - 1)


def _device(x, y, z, c):
    return (_mod(z, NZ), (_mod(x, NX) * NY + _mod(y, NY)) * 2 + c)


def _table():
    table = []
    for i in (0, 1, 2, -1):
        for j in (0, 1, 2, -1):
            dz = 0
            if TWIST and i and j and i + j:
                dz = min(i, j) if min(i, j) > 0 else -1
            table.append((i - dz, j - dz, dz))
    return table


TABLE = _table()


def _shift(k):
    if isinstance(k, int):
        return TABLE[k]
    i, j = k >> 2, k & 3
    if not TWIST:
        return i, j, 0
    low_i, low_j = jnp.where(i == 3, -1, i), jnp.where(j == 3, -1, j)
    both = jnp.where(jnp.minimum(low_i, low_j) > 0, jnp.minimum(low_i, low_j), -1)
    flat = (low_i == 0) | (low_j == 0) | (low_i + low_j == 0)
    dz = jnp.where(flat, 0, both)
    return i - dz, j - dz, dz


def kernel(
    x_ref, a_ref, s_ref, j_ref, out_ref, ev_ref,
    X, A, J1, ASM, PJ, H, T, SS, SR, WS, WB, WM, ACC, RS, RR, FS,
    lsem, xs, xr, as_, ar, js, jr, gs, gr, ss, sr, ws, wr, rs, rr, fs, fr,
):
    d, z = lax.axis_index("dom"), lax.axis_index("cls")
    c = d & 1
    y = (d >> 1) & 3
    x = d >> 3
    t = z if TWIST else 0

    def colour(i, j, core):
        return (_mod(x + t + i, NX) * NY + _mod(y + t + j, NY)) * 2 + core

    def cols(s):
        return pl.ds(pl.multiple_of(s * 256, 256), 256)

    def peer(k, core, sign=1):
        dx, dy, dz = _shift(k)
        return _device(x + sign * dx, y + sign * dy, z + sign * dz, core)

    def plane_peer(k, core):
        return _device(x + (k >> 2), y + (k & 3), z, core)

    def column_peer(h):
        if TWIST:
            return _device(x - h + 8, y - h + 8, z + h, c)
        return _device(x, y, z + h, c)

    def each(fn):
        fn(0, 1 - c)

        for k in range(1, 16):
            fn(k, 0)
            fn(k, 1)

    barrier = pltpu.get_barrier_semaphore()

    def greet(device):
        pl.semaphore_signal(barrier, inc=1, device_id=device, device_id_type=MESH)

    each(lambda k, core: greet(plane_peer(k, core)))
    for h in range(1, NZ):
        greet(_device(x, y, z + h, c))
    greeted = 31 + 7
    if TWIST:
        for dx, dy, dz in ((0, 0, 1), (1, 0, 1), (0, 1, 1), (0, 0, 2)):
            for sign in (1, -1):
                for core in (0, 1):
                    greet(_device(x + sign * dx, y + sign * dy, z + sign * dz, core))
                    greeted += 1
    pl.semaphore_wait(barrier, greeted)

    def send_j(k, core):
        s = colour((k >> 2), (k & 3), core)
        return pltpu.make_async_remote_copy(
            src_ref=j_ref.at[:, :, cols(s)], dst_ref=J1.at[d],
            send_sem=js, recv_sem=jr,
            device_id=plane_peer(k, core), device_id_type=MESH)

    def send_x(k, core):
        s = colour((k >> 2), (k & 3), core)
        return pltpu.make_async_remote_copy(
            src_ref=x_ref.at[:, cols(s)], dst_ref=X.at[2 * k + c],
            send_sem=xs, recv_sem=xr.at[k],
            device_id=peer(k, core), device_id_type=MESH)

    def send_a(k, core):
        return pltpu.make_async_remote_copy(
            src_ref=a_ref, dst_ref=A.at[2 * k + c],
            send_sem=as_, recv_sem=ar,
            device_id=peer(k, core), device_id_type=MESH)

    def all_of(buf, ssem, rsem, n=31):
        return pltpu.make_async_remote_copy(
            src_ref=buf.at[pl.ds(0, n)], dst_ref=buf.at[pl.ds(0, n)], send_sem=ssem, recv_sem=rsem,
            device_id=plane_peer(0, 1 - c), device_id_type=MESH)

    def send_s(k, core):
        return pltpu.make_async_remote_copy(
            src_ref=SS.at[2 * k + core], dst_ref=SR.at[2 * k + c],
            send_sem=ss, recv_sem=sr,
            device_id=peer(k, core, -1), device_id_type=MESH)

    def send_w(k, core):
        return pltpu.make_async_remote_copy(
            src_ref=WS, dst_ref=WB.at[2 * k + c],
            send_sem=ws, recv_sem=wr,
            device_id=peer(k, core), device_id_type=MESH)

    def send_g(h):
        return pltpu.make_async_remote_copy(
            src_ref=PJ.at[z], dst_ref=PJ.at[z], send_sem=gs, recv_sem=gr,
            device_id=column_peer(h), device_id_type=MESH)

    def send_r(h):
        return pltpu.make_async_remote_copy(
            src_ref=RS.at[h], dst_ref=RR.at[h], send_sem=rs, recv_sem=rr,
            device_id=column_peer(h), device_id_type=MESH)

    def send_f(k, core):
        q = (_mod(x + (k >> 2), NX) * NY + _mod(y + (k & 3), NY)) * 2 + core
        return pltpu.make_async_remote_copy(
            src_ref=FS.at[q], dst_ref=out_ref.at[:, :, cols(colour(0, 0, c))],
            send_sem=fs, recv_sem=fr,
            device_id=plane_peer(k, core), device_id_type=MESH)

    mine = colour(0, 0, c)
    own_x = pltpu.make_async_copy(x_ref.at[:, cols(mine)], X.at[c], lsem.at[0])
    own_j = pltpu.make_async_copy(j_ref.at[:, :, cols(mine)], J1.at[d], lsem.at[1])
    own_j.start()
    each(lambda k, core: send_j(k, core).start())
    each(lambda k, core: send_a(k, core).start())
    own_x.start()

    def start_x(lo, hi):
        for k in range(lo, hi):
            send_x(k, 0).start()
            send_x(k, 1).start()

    send_x(0, 1 - c).start()
    start_x(1, EARLY)
    A[c] = a_ref[...]

    own_j.wait()
    all_of(J1, js, jr).wait_recv()
    for q in range(32):
        for kk in range(2):
            ASM[kk * 64 + 2 * q : kk * 64 + 2 * q + 2, :] = J1[q, kk].astype(F32)
    PJ[z] = ASM[...].astype(BF16)
    for h in ORDER:
        send_g(h).start()
    start_x(EARLY, 16)

    all_of(PJ, gs, gr, 7).wait_recv()

    def halve(p, _):
        v = PJ[p].astype(F32)
        half = 0.5 * jnp.sum(v * v, axis=1, keepdims=True)
        H[p] = jnp.broadcast_to(half, (128, 128))
        return 0
    lax.fori_loop(0, NZ, halve, 0)

    own_x.wait()

    all_of(A, as_, ar).wait_recv()

    def score(k, _):
        @pl.when(k == 0)
        def _():
            all_of(X, xs, xr.at[0], 1).wait_recv()

        @pl.when(k != 0)
        def _():
            all_of(X, xs, xr.at[k], 2).wait_recv()

        rows = X[pl.ds(2 * k, 2)].reshape(256, 256)
        T[...] = lax.dot_general(
            PJ[...].reshape(1024, 256), rows, (((1,), (1,)), ((), ())), preferred_element_type=F32)
        for core in range(2):
            ids = jnp.broadcast_to(A[2 * k + core], (64, 128))
            total = jnp.zeros((64, 128), F32)
            for m in range(16):
                part = T[m * 64 : (m + 1) * 64, core * 128 : (core + 1) * 128]
                half = H[m // 2, (m % 2) * 64 : (m % 2) * 64 + 64, :]
                total = jnp.where(ids == m, part - half, total)
            SS[2 * k + core] = total
        for core in range(2):
            @pl.when((k != 0) | (c != core))
            def _():
                send_s(k, core).start()
        return 0
    lax.fori_loop(0, 16, score, 0)

    all_of(SR, ss, sr).wait_recv()

    def gather(k, total):
        return total + SR[2 * k] + SR[2 * k + 1]
    total = lax.fori_loop(1, 16, gather, SS[c] + SR[1 - c])
    scores = total * s_ref[...].astype(F32)
    largest = jnp.max(scores, axis=0, keepdims=True)
    expo = jnp.exp(scores - largest)
    sums = jnp.sum(expo, axis=0, keepdims=True)
    weight = (expo / sums).astype(BF16)
    WS[...] = weight
    WB[c] = weight
    each(lambda k, core: send_w(k, core).start())
    ev_ref[...] = largest + jnp.log(sums)

    ACC[...] = jnp.zeros_like(ACC)
    all_of(WB, ws, wr).wait_recv()

    def accumulate(k, _):
        for core in range(2):
            ids = jnp.broadcast_to(A[2 * k + core], (64, 128))
            w = WB[2 * k + core].astype(F32)
            for m in range(16):
                WM[m * 64 : (m + 1) * 64, core * 128 : (core + 1) * 128] = jnp.where(ids == m, w, 0.0).astype(BF16)
        rows = X[pl.ds(2 * k, 2)].reshape(256, 256)
        ACC[...] += jnp.dot(WM[...], rows, preferred_element_type=F32)
        return 0
    lax.fori_loop(0, 16, accumulate, 0)

    for h in ORDER:
        p = _mod(z + h, NZ)
        RS[h] = ACC[pl.ds(pl.multiple_of(p * 128, 128), 128), :].astype(BF16)
        send_r(h).start()
    final = ACC[pl.ds(pl.multiple_of(z * 128, 128), 128), :]
    all_of(RR, rs, rr, 7).wait_recv()
    for h in range(1, NZ):
        final = final + RR[h].astype(F32)
    ASM[...] = final
    for q in range(32):
        for kk in range(2):
            FS[q, kk] = ASM[kk * 64 + 2 * q : kk * 64 + 2 * q + 2, :]
    each(lambda k, core: send_f(k, core).start())
    out_ref[:, :, cols(mine)] = FS[d]
    all_of(FS, fs, fr).wait_recv()

    for buf, sem in ((J1, js), (A, as_), (X, xs), (SS, ss), (WB, ws), (FS, fs)):
        all_of(buf, sem, sem).wait_send()
    all_of(PJ, gs, gr, 7).wait_send()
    all_of(RS, rs, rr, 7).wait_send()


def on_device(particles, assign, inv_sigma, projections):
    dma = pltpu.SemaphoreType.DMA
    vmem = pltpu.VMEM
    sums, evidence = pl.pallas_call(
        kernel,
        name="estep",
        out_shape=(
            jax.ShapeDtypeStruct((2, 2, 8192), F32),
            jax.ShapeDtypeStruct((1, 128), F32),
        ),
        in_specs=[
            pl.BlockSpec(memory_space=pl.ANY),
            pl.BlockSpec(memory_space=pltpu.VMEM),
            pl.BlockSpec(memory_space=pltpu.VMEM),
            pl.BlockSpec(memory_space=pl.ANY),
        ],
        out_specs=(
            pl.BlockSpec(memory_space=pltpu.VMEM),
            pl.BlockSpec(memory_space=pltpu.VMEM),
        ),
        scratch_shapes=[
            vmem((32, 128, 256), BF16),
            vmem((32, 1, 128), jnp.int32),
            vmem((32, 2, 2, 256), BF16),
            vmem((128, 256), F32),
            vmem((8, 128, 256), BF16),
            vmem((8, 128, 128), F32),
            vmem((1024, 256), F32),
            vmem((32, 64, 128), F32),
            vmem((32, 64, 128), F32),
            vmem((64, 128), BF16),
            vmem((32, 64, 128), BF16),
            vmem((1024, 256), BF16),
            vmem((1024, 256), F32),
            vmem((8, 128, 256), BF16),
            vmem((8, 128, 256), BF16),
            vmem((32, 2, 2, 256), F32),
            dma((2,)),
            dma, dma((16,)),
            dma, dma,
            dma, dma,
            dma, dma,
            dma, dma,
            dma, dma,
            dma, dma,
            dma, dma,
        ],
        compiler_params=pltpu.CompilerParams(collective_id=0, has_side_effects=True),
    )(particles, assign.reshape(1, 128), inv_sigma.reshape(1, 128), projections)
    return sums, evidence.reshape(128)


def solution(mesh):
    return jax.shard_map(
        on_device,
        mesh=mesh,
        in_specs=(
            P(("cls", "dom"), None),
            P(("cls", "dom"), None),
            P(("cls", "dom")),
            P("cls", "dom", None),
        ),
        out_specs=(P("cls", "dom", None), P(("cls", "dom"))),
        check_vma=False,
    )
```

```python
import functools

import jax
import jax.numpy as jnp
from jax import lax
from jax.experimental import pallas as pl
from jax.experimental.pallas import tpu as pltpu
from jax.sharding import PartitionSpec as P

MESH = pl.DeviceIdType.MESH
TWIST = True
EARLY = 7
FAR_FIRST = (2, -2, 3, -3, 4, 1, -1)
PLANES = (0, 1, -1, 2, -2, 3, -3, 4)
SLOT = {h: q for q, h in enumerate(PLANES)}
NX, NY, NZ = 4, 4, 8
F32 = jnp.float32
BF16 = jnp.bfloat16


def _mod(v, n):
    return v % n if isinstance(v, int) else v & (n - 1)


def _device(x, y, z, c):
    return (_mod(z, NZ), (_mod(x, NX) * NY + _mod(y, NY)) * 2 + c)


def _table():
    table = []
    for i in (0, 1, 2, -1):
        for j in (0, 1, 2, -1):
            dz = 0
            if TWIST and i and j and i + j:
                dz = min(i, j) if min(i, j) > 0 else -1
            table.append((i - dz, j - dz, dz))
    return table


TABLE = _table()


def _shift(k):
    if isinstance(k, int):
        return TABLE[k]
    i, j = k >> 2, k & 3
    if not TWIST:
        return i, j, 0
    low_i, low_j = jnp.where(i == 3, -1, i), jnp.where(j == 3, -1, j)
    both = jnp.where(jnp.minimum(low_i, low_j) > 0, jnp.minimum(low_i, low_j), -1)
    flat = (low_i == 0) | (low_j == 0) | (low_i + low_j == 0)
    dz = jnp.where(flat, 0, both)
    return i - dz, j - dz, dz


def kernel(
    x_ref, a_ref, s_ref, j_ref, out_ref, ev_ref,
    X, A, J1, ASM, PJ, H, T, SS, SR, WS, WB, WM, ACC, RS, RR, FS,
    lsem, xs, xr, as_, ar, js, jr, gs, gr, ss, sr, ws, wr, rs, rr, fs, fr,
):
    d, z = lax.axis_index("dom"), lax.axis_index("cls")
    c = d & 1
    y = (d >> 1) & 3
    x = d >> 3
    t = z if TWIST else 0

    def colour(i, j, core):
        return (_mod(x + t + i, NX) * NY + _mod(y + t + j, NY)) * 2 + core

    def cols(s):
        return pl.ds(pl.multiple_of(s * 256, 256), 256)

    def peer(k, core, sign=1):
        dx, dy, dz = _shift(k)
        return _device(x + sign * dx, y + sign * dy, z + sign * dz, core)

    def plane_peer(k, core):
        return _device(x + (k >> 2), y + (k & 3), z, core)

    def column_peer(h):
        if TWIST:
            return _device(x - h, y - h, z + h, c)
        return _device(x, y, z + h, c)

    def each(fn):
        fn(0, 1 - c)

        for k in range(1, 16):
            fn(k, 0)
            fn(k, 1)

    barrier = pltpu.get_barrier_semaphore()

    def greet(device):
        pl.semaphore_signal(barrier, inc=1, device_id=device, device_id_type=MESH)

    each(lambda k, core: greet(plane_peer(k, core)))
    for h in range(1, NZ):
        greet(_device(x, y, z + h, c))
    greeted = 31 + 7
    if TWIST:
        for dx, dy, dz in ((0, 0, 1), (1, 0, 1), (0, 1, 1), (0, 0, 2)):
            for sign in (1, -1):
                for core in (0, 1):
                    greet(_device(x + sign * dx, y + sign * dy, z + sign * dz, core))
                    greeted += 1
    pl.semaphore_wait(barrier, greeted)

    def send_j(k, core):
        s = colour((k >> 2), (k & 3), core)
        return pltpu.make_async_remote_copy(
            src_ref=j_ref.at[:, :, cols(s)], dst_ref=J1.at[d],
            send_sem=js, recv_sem=jr,
            device_id=plane_peer(k, core), device_id_type=MESH)

    def send_x(k, core):
        s = colour((k >> 2), (k & 3), core)
        return pltpu.make_async_remote_copy(
            src_ref=x_ref.at[:, cols(s)], dst_ref=X.at[2 * k + c],
            send_sem=xs, recv_sem=xr.at[k],
            device_id=peer(k, core), device_id_type=MESH)

    def send_a(k, core):
        return pltpu.make_async_remote_copy(
            src_ref=a_ref, dst_ref=A.at[2 * k + c],
            send_sem=as_, recv_sem=ar,
            device_id=peer(k, core), device_id_type=MESH)

    def all_of(buf, ssem, rsem, n=31):
        return pltpu.make_async_remote_copy(
            src_ref=buf.at[pl.ds(0, n)], dst_ref=buf.at[pl.ds(0, n)], send_sem=ssem, recv_sem=rsem,
            device_id=plane_peer(0, 1 - c), device_id_type=MESH)

    def send_s(k, core):
        return pltpu.make_async_remote_copy(
            src_ref=SS.at[2 * k + core], dst_ref=SR.at[2 * k + c],
            send_sem=ss, recv_sem=sr,
            device_id=peer(k, core, -1), device_id_type=MESH)

    def send_w(k, core):
        return pltpu.make_async_remote_copy(
            src_ref=WS, dst_ref=WB.at[2 * k + c],
            send_sem=ws, recv_sem=wr.at[k],
            device_id=peer(k, core), device_id_type=MESH)

    def send_g(h):
        q = SLOT[4 if h == 4 else -h]
        return pltpu.make_async_remote_copy(
            src_ref=PJ.at[0], dst_ref=PJ.at[q], send_sem=gs, recv_sem=gr.at[q],
            device_id=column_peer(h), device_id_type=MESH)

    def send_r(h):
        h = h % NZ
        return pltpu.make_async_remote_copy(
            src_ref=RS.at[h], dst_ref=RR.at[h], send_sem=rs, recv_sem=rr,
            device_id=column_peer(h), device_id_type=MESH)

    def send_f(k, core):
        q = (_mod(x + (k >> 2), NX) * NY + _mod(y + (k & 3), NY)) * 2 + core
        return pltpu.make_async_remote_copy(
            src_ref=FS.at[q], dst_ref=out_ref.at[:, :, cols(colour(0, 0, c))],
            send_sem=fs, recv_sem=fr,
            device_id=plane_peer(k, core), device_id_type=MESH)

    mine = colour(0, 0, c)
    own_x = pltpu.make_async_copy(x_ref.at[:, cols(mine)], X.at[c], lsem.at[0])
    own_j = pltpu.make_async_copy(j_ref.at[:, :, cols(mine)], J1.at[d], lsem.at[1])
    own_j.start()
    each(lambda k, core: send_j(k, core).start())
    each(lambda k, core: send_a(k, core).start())
    own_x.start()

    def start_x(lo, hi):
        for k in range(lo, hi):
            send_x(k, 0).start()
            send_x(k, 1).start()

    send_x(0, 1 - c).start()
    start_x(1, EARLY)
    A[c] = a_ref[...]

    own_j.wait()
    all_of(J1, js, jr).wait_recv()
    for q in range(32):
        for kk in range(2):
            ASM[kk * 64 + 2 * q : kk * 64 + 2 * q + 2, :] = J1[q, kk].astype(F32)
    PJ[0] = ASM[...].astype(BF16)

    def halve(lo, hi):
        for q in range(lo, hi):
            v = PJ[q].astype(F32)
            H[q] = jnp.broadcast_to(0.5 * jnp.sum(v * v, axis=1, keepdims=True), (128, 128))

    for h in FAR_FIRST:
        send_g(h).start()
    start_x(EARLY, 16)
    halve(0, 1)
    for h in FAR_FIRST:
        send_g(h).wait_recv()
        q = SLOT[4 if h == 4 else -h]
        halve(q, q + 1)

    own_x.wait()

    all_of(A, as_, ar).wait_recv()

    def choose(total, k, core, lo, hi):
        ids = jnp.broadcast_to(A[2 * k + core], (64, 128))
        for q in range(lo, hi):
            for kk in range(2):
                at = (q - lo) * 128 + kk * 64
                part = T[at : at + 64, core * 128 : (core + 1) * 128]
                half = H[q, kk * 64 : kk * 64 + 64, :]
                total = jnp.where(ids == 2 * ((z + PLANES[q]) & 7) + kk, part - half, total)
        return total

    def score(k, _):
        @pl.when(k == 0)
        def _():
            all_of(X, xs, xr.at[0], 1).wait_recv()

        @pl.when(k != 0)
        def _():
            all_of(X, xs, xr.at[k], 2).wait_recv()

        rows = X[pl.ds(2 * k, 2)].reshape(256, 256)
        T[...] = lax.dot_general(
            PJ[...].reshape(1024, 256), rows, (((1,), (1,)), ((), ())), preferred_element_type=F32)
        for core in range(2):
            SS[2 * k + core] = choose(jnp.zeros((64, 128), F32), k, core, 0, 8)
        for core in range(2):
            @pl.when((k != 0) | (c != core))
            def _():
                send_s(k, core).start()
        return 0
    lax.fori_loop(0, 16, score, 0)

    all_of(SR, ss, sr).wait_recv()

    def gather(k, total):
        return total + SR[2 * k] + SR[2 * k + 1]
    total = lax.fori_loop(1, 16, gather, SS[c] + SR[1 - c])
    scores = total * s_ref[...].astype(F32)
    largest = jnp.max(scores, axis=0, keepdims=True)
    expo = jnp.exp(scores - largest)
    sums = jnp.sum(expo, axis=0, keepdims=True)
    weight = (expo / sums).astype(BF16)
    WS[...] = weight
    WB[c] = weight
    each(lambda k, core: send_w(k, core).start())
    ev_ref[...] = largest + jnp.log(sums)

    def accumulate(n, group, wait):
        for k in (2 * n, 2 * n + 1):
            if wait:
                @pl.when(k == 0)
                def _():
                    all_of(WB, ws, wr.at[0], 1).wait_recv()

                @pl.when(k != 0)
                def _():
                    all_of(WB, ws, wr.at[k], 2).wait_recv()
        for part in range(4):
            ids = jnp.broadcast_to(A[4 * n + part], (64, 128))
            w = WB[4 * n + part].astype(F32)
            for q in range(4):
                for kk in range(2):
                    at = q * 128 + kk * 64
                    live = ids == 2 * ((z + PLANES[4 * group + q]) & 7) + kk
                    WM[at : at + 64, part * 128 : (part + 1) * 128] = jnp.where(live, w, 0.0).astype(BF16)
        rows = X[pl.ds(4 * n, 4)].reshape(512, 256)
        ACC[group] += jnp.dot(WM[...], rows, preferred_element_type=F32)
        return 0

    ACC[...] = jnp.zeros_like(ACC)
    for group in (1, 0):
        lax.fori_loop(0, 8, lambda n, _, group=group: accumulate(n, group, group == 1), 0)
        for q in (3, 2, 1, 0):
            h = PLANES[4 * group + q]
            if h:
                RS[h % NZ] = ACC[group, q * 128 : (q + 1) * 128, :].astype(BF16)
                send_r(h).start()
    final = ACC[0, 0:128, :]
    all_of(RR, rs, rr, 7).wait_recv()
    for h in range(1, NZ):
        final = final + RR[h].astype(F32)
    ASM[...] = final
    for q in range(32):
        for kk in range(2):
            FS[q, kk] = ASM[kk * 64 + 2 * q : kk * 64 + 2 * q + 2, :]
    each(lambda k, core: send_f(k, core).start())
    out_ref[:, :, cols(mine)] = FS[d]
    all_of(FS, fs, fr).wait_recv()

    for buf, sem in ((J1, js), (A, as_), (X, xs), (SS, ss), (WB, ws), (FS, fs)):
        all_of(buf, sem, sem).wait_send()
    all_of(PJ, gs, gs, 7).wait_send()
    all_of(RS, rs, rr, 7).wait_send()


def deliver(sums_ref, evidence_ref, out_ref, ev_ref):
    out_ref[...] = sums_ref[...]
    ev_ref[...] = evidence_ref[...]


def on_device(particles, assign, inv_sigma, projections):
    dma = pltpu.SemaphoreType.DMA
    vmem = pltpu.VMEM
    sums, evidence = pl.pallas_call(
        kernel,
        name="estep",
        out_shape=(
            jax.ShapeDtypeStruct((2, 2, 8192), F32),
            jax.ShapeDtypeStruct((1, 128), F32),
        ),
        in_specs=[
            pl.BlockSpec(memory_space=pl.ANY),
            pl.BlockSpec(memory_space=pltpu.VMEM),
            pl.BlockSpec(memory_space=pltpu.VMEM),
            pl.BlockSpec(memory_space=pl.ANY),
        ],
        out_specs=(
            pl.BlockSpec(memory_space=pltpu.VMEM),
            pl.BlockSpec(memory_space=pltpu.VMEM),
        ),
        scratch_shapes=[
            vmem((32, 128, 256), BF16),
            vmem((32, 1, 128), jnp.int32),
            vmem((32, 2, 2, 256), BF16),
            vmem((128, 256), F32),
            vmem((8, 128, 256), BF16),
            vmem((8, 128, 128), F32),
            vmem((1024, 256), F32),
            vmem((32, 64, 128), F32),
            vmem((32, 64, 128), F32),
            vmem((64, 128), BF16),
            vmem((32, 64, 128), BF16),
            vmem((512, 512), BF16),
            vmem((2, 512, 256), F32),
            vmem((8, 128, 256), BF16),
            vmem((8, 128, 256), BF16),
            vmem((32, 2, 2, 256), F32),
            dma((2,)),
            dma, dma((16,)),
            dma, dma,
            dma, dma,
            dma, dma((8,)),
            dma, dma,
            dma, dma((16,)),
            dma, dma,
            dma, dma,
        ],
        compiler_params=pltpu.CompilerParams(collective_id=0, has_side_effects=True),
    )(particles, assign.reshape(1, 128), inv_sigma.reshape(1, 128), projections)
    sums, evidence = pl.pallas_call(
        deliver,
        name="deliver",
        out_shape=(
            jax.ShapeDtypeStruct((2, 2, 8192), F32),
            jax.ShapeDtypeStruct((1, 128), F32),
        ),
    )(sums, evidence)
    return sums, evidence.reshape(128)


def solution(mesh):
    return jax.shard_map(
        on_device,
        mesh=mesh,
        in_specs=(
            P(("cls", "dom"), None),
            P(("cls", "dom"), None),
            P(("cls", "dom")),
            P("cls", "dom", None),
        ),
        out_specs=(P("cls", "dom", None), P(("cls", "dom"))),
        check_vma=False,
    )
```

```python
import functools

import jax
import jax.numpy as jnp
from jax import lax
from jax.experimental import pallas as pl
from jax.experimental.pallas import tpu as pltpu
from jax.sharding import PartitionSpec as P

MESH = pl.DeviceIdType.MESH
TWIST = True
EARLY = 7
FAR_FIRST = (2, -2, 3, -3, 4, 1, -1)
PLANES = (0, 1, -1, 4, 2, -2, 3, -3)
SLOT = {h: q for q, h in enumerate(PLANES)}
NX, NY, NZ = 4, 4, 8
F32 = jnp.float32
BF16 = jnp.bfloat16


def _mod(v, n):
    return v % n if isinstance(v, int) else v & (n - 1)


def _device(x, y, z, c):
    return (_mod(z, NZ), (_mod(x, NX) * NY + _mod(y, NY)) * 2 + c)


def _table():
    table = []
    for i in (0, 1, 2, -1):
        for j in (0, 1, 2, -1):
            dz = 0
            if TWIST and i and j and i + j:
                dz = min(i, j) if min(i, j) > 0 else -1
            table.append((i - dz, j - dz, dz))
    return table


TABLE = _table()


def _shift(k):
    if isinstance(k, int):
        return TABLE[k]
    i, j = k >> 2, k & 3
    if not TWIST:
        return i, j, 0
    low_i, low_j = jnp.where(i == 3, -1, i), jnp.where(j == 3, -1, j)
    both = jnp.where(jnp.minimum(low_i, low_j) > 0, jnp.minimum(low_i, low_j), -1)
    flat = (low_i == 0) | (low_j == 0) | (low_i + low_j == 0)
    dz = jnp.where(flat, 0, both)
    return i - dz, j - dz, dz


def kernel(
    x_ref, a_ref, s_ref, j_ref, out_ref, ev_ref,
    X, A, J1, ASM, PJ, H, T, SS, SR, WS, WB, WM, ACC, RS, RR, FS,
    lsem, xs, xr, as_, ar, js, jr, gs, gr, ss, sr, ws, wr, rs, rr, fs, fr,
):
    d, z = lax.axis_index("dom"), lax.axis_index("cls")
    c = d & 1
    y = (d >> 1) & 3
    x = d >> 3
    t = z if TWIST else 0

    def colour(i, j, core):
        return (_mod(x + t + i, NX) * NY + _mod(y + t + j, NY)) * 2 + core

    def cols(s):
        return pl.ds(pl.multiple_of(s * 256, 256), 256)

    def peer(k, core, sign=1):
        dx, dy, dz = _shift(k)
        return _device(x + sign * dx, y + sign * dy, z + sign * dz, core)

    def plane_peer(k, core):
        return _device(x + (k >> 2), y + (k & 3), z, core)

    def column_peer(h):
        if TWIST:
            return _device(x - h, y - h, z + h, c)
        return _device(x, y, z + h, c)

    def each(fn):
        fn(0, 1 - c)

        for k in range(1, 16):
            fn(k, 0)
            fn(k, 1)

    barrier = pltpu.get_barrier_semaphore()

    def greet(device):
        pl.semaphore_signal(barrier, inc=1, device_id=device, device_id_type=MESH)

    each(lambda k, core: greet(plane_peer(k, core)))
    for h in range(1, NZ):
        greet(_device(x, y, z + h, c))
    greeted = 31 + 7
    if TWIST:
        for dx, dy, dz in ((0, 0, 1), (1, 0, 1), (0, 1, 1), (0, 0, 2)):
            for sign in (1, -1):
                for core in (0, 1):
                    greet(_device(x + sign * dx, y + sign * dy, z + sign * dz, core))
                    greeted += 1
    pl.semaphore_wait(barrier, greeted)

    def send_j(k, core):
        s = colour((k >> 2), (k & 3), core)
        return pltpu.make_async_remote_copy(
            src_ref=j_ref.at[:, :, cols(s)], dst_ref=J1.at[d],
            send_sem=js, recv_sem=jr,
            device_id=plane_peer(k, core), device_id_type=MESH)

    def send_x(k, core):
        s = colour((k >> 2), (k & 3), core)
        return pltpu.make_async_remote_copy(
            src_ref=x_ref.at[:, cols(s)], dst_ref=X.at[2 * k + c],
            send_sem=xs, recv_sem=xr.at[k],
            device_id=peer(k, core), device_id_type=MESH)

    def send_a(k, core):
        return pltpu.make_async_remote_copy(
            src_ref=a_ref, dst_ref=A.at[2 * k + c],
            send_sem=as_, recv_sem=ar,
            device_id=peer(k, core), device_id_type=MESH)

    def all_of(buf, ssem, rsem, n=31):
        return pltpu.make_async_remote_copy(
            src_ref=buf.at[pl.ds(0, n)], dst_ref=buf.at[pl.ds(0, n)], send_sem=ssem, recv_sem=rsem,
            device_id=plane_peer(0, 1 - c), device_id_type=MESH)

    def send_s(k, core):
        return pltpu.make_async_remote_copy(
            src_ref=SS.at[2 * k + core], dst_ref=SR.at[2 * k + c],
            send_sem=ss, recv_sem=sr,
            device_id=peer(k, core, -1), device_id_type=MESH)

    def send_w(k, core):
        return pltpu.make_async_remote_copy(
            src_ref=WS, dst_ref=WB.at[2 * k + c],
            send_sem=ws, recv_sem=wr.at[k],
            device_id=peer(k, core), device_id_type=MESH)

    def send_g(h):
        q = SLOT[4 if h == 4 else -h]
        return pltpu.make_async_remote_copy(
            src_ref=PJ.at[0], dst_ref=PJ.at[q], send_sem=gs, recv_sem=gr.at[q],
            device_id=column_peer(h), device_id_type=MESH)

    def send_r(h):
        h = h % NZ
        return pltpu.make_async_remote_copy(
            src_ref=RS.at[h], dst_ref=RR.at[h], send_sem=rs, recv_sem=rr,
            device_id=column_peer(h), device_id_type=MESH)

    def send_f(k, core):
        q = (_mod(x + (k >> 2), NX) * NY + _mod(y + (k & 3), NY)) * 2 + core
        return pltpu.make_async_remote_copy(
            src_ref=FS.at[q], dst_ref=out_ref.at[:, :, cols(colour(0, 0, c))],
            send_sem=fs, recv_sem=fr,
            device_id=plane_peer(k, core), device_id_type=MESH)

    mine = colour(0, 0, c)
    own_x = pltpu.make_async_copy(x_ref.at[:, cols(mine)], X.at[c], lsem.at[0])
    own_j = pltpu.make_async_copy(j_ref.at[:, :, cols(mine)], J1.at[d], lsem.at[1])
    own_j.start()
    each(lambda k, core: send_j(k, core).start())
    each(lambda k, core: send_a(k, core).start())
    own_x.start()

    def start_x(lo, hi):
        for k in range(lo, hi):
            send_x(k, 0).start()
            send_x(k, 1).start()

    send_x(0, 1 - c).start()
    start_x(1, EARLY)
    A[c] = a_ref[...]

    own_j.wait()
    all_of(J1, js, jr).wait_recv()
    for q in range(32):
        for kk in range(2):
            ASM[kk * 64 + 2 * q : kk * 64 + 2 * q + 2, :] = J1[q, kk].astype(F32)
    PJ[0] = ASM[...].astype(BF16)

    def halve(lo, hi):
        for q in range(lo, hi):
            v = PJ[q].astype(F32)
            H[q] = jnp.broadcast_to(0.5 * jnp.sum(v * v, axis=1, keepdims=True), (128, 128))

    for h in FAR_FIRST:
        send_g(h).start()
    start_x(EARLY, 16)
    halve(0, 1)
    for h in FAR_FIRST:
        send_g(h).wait_recv()
        q = SLOT[4 if h == 4 else -h]
        halve(q, q + 1)

    own_x.wait()

    all_of(A, as_, ar).wait_recv()

    def choose(total, k, core, lo, hi):
        ids = jnp.broadcast_to(A[2 * k + core], (8, 128))
        for q in range(lo, hi):
            for kk in range(2):
                live = ids == 2 * ((z + PLANES[q]) & 7) + kk
                for g in range(8):
                    at = (q - lo) * 128 + kk * 64 + 8 * g
                    part = T[at : at + 8, core * 128 : (core + 1) * 128]
                    half = H[q, kk * 64 + 8 * g : kk * 64 + 8 * g + 8, :]
                    total[g] = jnp.where(live, part - half, total[g])
        return total

    def score(k, _):
        @pl.when(k == 0)
        def _():
            all_of(X, xs, xr.at[0], 1).wait_recv()

        @pl.when(k != 0)
        def _():
            all_of(X, xs, xr.at[k], 2).wait_recv()

        rows = X[pl.ds(2 * k, 2)].reshape(256, 256)
        T[...] = lax.dot_general(
            PJ[...].reshape(1024, 256), rows, (((1,), (1,)), ((), ())), preferred_element_type=F32)
        for core in range(2):
            total = choose([jnp.zeros((8, 128), F32)] * 8, k, core, 0, 8)
            for g in range(8):
                SS[2 * k + core, 8 * g : 8 * g + 8, :] = total[g]
        for core in range(2):
            @pl.when((k != 0) | (c != core))
            def _():
                send_s(k, core).start()
        return 0
    lax.fori_loop(0, 16, score, 0)

    all_of(SR, ss, sr).wait_recv()

    def gather(k, total):
        return total + SR[2 * k] + SR[2 * k + 1]
    total = lax.fori_loop(1, 16, gather, SS[c] + SR[1 - c])
    scores = total * s_ref[...].astype(F32)
    largest = jnp.max(scores, axis=0, keepdims=True)
    expo = jnp.exp(scores - largest)
    sums = jnp.sum(expo, axis=0, keepdims=True)
    weight = (expo / sums).astype(BF16)
    WS[...] = weight
    WB[c] = weight
    each(lambda k, core: send_w(k, core).start())
    ev_ref[...] = largest + jnp.log(sums)

    def accumulate(n, group, wait):
        for k in (2 * n, 2 * n + 1):
            if wait:
                @pl.when(k == 0)
                def _():
                    all_of(WB, ws, wr.at[0], 1).wait_recv()

                @pl.when(k != 0)
                def _():
                    all_of(WB, ws, wr.at[k], 2).wait_recv()
        for part in range(4):
            ids = jnp.broadcast_to(A[4 * n + part], (8, 128))
            w = WB[4 * n + part].astype(F32)
            for q in range(4):
                for kk in range(2):
                    at = q * 128 + kk * 64
                    live = ids == 2 * ((z + PLANES[4 * group + q]) & 7) + kk
                    for g in range(4):
                        pair = [jnp.where(live, w[16 * g + 8 * i : 16 * g + 8 * i + 8], 0.0) for i in range(2)]
                        WM[at + 16 * g : at + 16 * g + 16, part * 128 : (part + 1) * 128] = (
                            jnp.concatenate(pair, axis=0).astype(BF16))
        rows = X[pl.ds(4 * n, 4)].reshape(512, 256)
        ACC[group] += jnp.dot(WM[...], rows, preferred_element_type=F32)
        return 0

    ACC[...] = jnp.zeros_like(ACC)
    for group in (1, 0):
        lax.fori_loop(0, 8, lambda n, _, group=group: accumulate(n, group, group == 1), 0)
        for q in (3, 2, 1, 0):
            h = PLANES[4 * group + q]
            if h:
                RS[h % NZ] = ACC[group, q * 128 : (q + 1) * 128, :].astype(BF16)
                send_r(h).start()
    final = ACC[0, 0:128, :]
    all_of(RR, rs, rr, 7).wait_recv()
    for h in range(1, NZ):
        final = final + RR[h].astype(F32)
    ASM[...] = final
    for q in range(32):
        for kk in range(2):
            FS[q, kk] = ASM[kk * 64 + 2 * q : kk * 64 + 2 * q + 2, :]
    each(lambda k, core: send_f(k, core).start())
    out_ref[:, :, cols(mine)] = FS[d]
    all_of(FS, fs, fr).wait_recv()

    for buf, sem in ((J1, js), (A, as_), (X, xs), (SS, ss), (WB, ws), (FS, fs)):
        all_of(buf, sem, sem).wait_send()
    all_of(PJ, gs, gs, 7).wait_send()
    all_of(RS, rs, rr, 7).wait_send()


def deliver(sums_ref, evidence_ref, out_ref, ev_ref):
    out_ref[...] = sums_ref[...]
    ev_ref[...] = evidence_ref[...]


def on_device(particles, assign, inv_sigma, projections):
    dma = pltpu.SemaphoreType.DMA
    vmem = pltpu.VMEM
    sums, evidence = pl.pallas_call(
        kernel,
        name="estep",
        out_shape=(
            jax.ShapeDtypeStruct((2, 2, 8192), F32),
            jax.ShapeDtypeStruct((1, 128), F32),
        ),
        in_specs=[
            pl.BlockSpec(memory_space=pl.ANY),
            pl.BlockSpec(memory_space=pltpu.VMEM),
            pl.BlockSpec(memory_space=pltpu.VMEM),
            pl.BlockSpec(memory_space=pl.ANY),
        ],
        out_specs=(
            pl.BlockSpec(memory_space=pltpu.VMEM),
            pl.BlockSpec(memory_space=pltpu.VMEM),
        ),
        scratch_shapes=[
            vmem((32, 128, 256), BF16),
            vmem((32, 1, 128), jnp.int32),
            vmem((32, 2, 2, 256), BF16),
            vmem((128, 256), F32),
            vmem((8, 128, 256), BF16),
            vmem((8, 128, 128), F32),
            vmem((1024, 256), F32),
            vmem((32, 64, 128), F32),
            vmem((32, 64, 128), F32),
            vmem((64, 128), BF16),
            vmem((32, 64, 128), BF16),
            vmem((512, 512), BF16),
            vmem((2, 512, 256), F32),
            vmem((8, 128, 256), BF16),
            vmem((8, 128, 256), BF16),
            vmem((32, 2, 2, 256), F32),
            dma((2,)),
            dma, dma((16,)),
            dma, dma,
            dma, dma,
            dma, dma((8,)),
            dma, dma,
            dma, dma((16,)),
            dma, dma,
            dma, dma,
        ],
        compiler_params=pltpu.CompilerParams(collective_id=0, has_side_effects=True),
    )(particles, assign.reshape(1, 128), inv_sigma.reshape(1, 128), projections)
    sums, evidence = pl.pallas_call(
        deliver,
        name="deliver",
        out_shape=(
            jax.ShapeDtypeStruct((2, 2, 8192), F32),
            jax.ShapeDtypeStruct((1, 128), F32),
        ),
    )(sums, evidence)
    return sums, evidence.reshape(128)


def solution(mesh):
    return jax.shard_map(
        on_device,
        mesh=mesh,
        in_specs=(
            P(("cls", "dom"), None),
            P(("cls", "dom"), None),
            P(("cls", "dom")),
            P("cls", "dom", None),
        ),
        out_specs=(P("cls", "dom", None), P(("cls", "dom"))),
        check_vma=False,
    )
```

```python
import functools

import jax
import jax.numpy as jnp
from jax import lax
from jax.experimental import pallas as pl
from jax.experimental.pallas import tpu as pltpu
from jax.sharding import PartitionSpec as P

MESH = pl.DeviceIdType.MESH
TWIST = True
EARLY = 7
FAR_FIRST = (2, -2, 3, -3, 4, 1, -1)
PLANES = (0, 1, -1, 4, 2, -2, 3, -3)
SLOT = {h: q for q, h in enumerate(PLANES)}
NX, NY, NZ = 4, 4, 8
F32 = jnp.float32
BF16 = jnp.bfloat16


def _mod(v, n):
    return v % n if isinstance(v, int) else v & (n - 1)


def _device(x, y, z, c):
    return (_mod(z, NZ), (_mod(x, NX) * NY + _mod(y, NY)) * 2 + c)


def _table():
    table = []
    for i in (0, 1, 2, -1):
        for j in (0, 1, 2, -1):
            dz = 0
            if TWIST and i and j and i + j:
                dz = min(i, j) if min(i, j) > 0 else -1
            table.append((i - dz, j - dz, dz))
    return table


TABLE = _table()


def _shift(k):
    if isinstance(k, int):
        return TABLE[k]
    i, j = k >> 2, k & 3
    if not TWIST:
        return i, j, 0
    low_i, low_j = jnp.where(i == 3, -1, i), jnp.where(j == 3, -1, j)
    both = jnp.where(jnp.minimum(low_i, low_j) > 0, jnp.minimum(low_i, low_j), -1)
    flat = (low_i == 0) | (low_j == 0) | (low_i + low_j == 0)
    dz = jnp.where(flat, 0, both)
    return i - dz, j - dz, dz


def kernel(
    x_ref, a_ref, s_ref, j_ref, out_ref, ev_ref,
    X, A, J1, ASM, PJ, H, T, SS, SR, WS, WB, WM, ACC, RS, RR, FS,
    lsem, xs, xr, as_, ar, js, jr, gs, gr, ss, sr, ws, wr, rs, rr, fs, fr,
):
    d, z = lax.axis_index("dom"), lax.axis_index("cls")
    c = d & 1
    y = (d >> 1) & 3
    x = d >> 3
    t = z if TWIST else 0

    def colour(i, j, core):
        return (_mod(x + t + i, NX) * NY + _mod(y + t + j, NY)) * 2 + core

    def cols(s):
        return pl.ds(pl.multiple_of(s * 256, 256), 256)

    def peer(k, core, sign=1):
        dx, dy, dz = _shift(k)
        return _device(x + sign * dx, y + sign * dy, z + sign * dz, core)

    def plane_peer(k, core):
        return _device(x + (k >> 2), y + (k & 3), z, core)

    def column_peer(h):
        if TWIST:
            return _device(x - h, y - h, z + h, c)
        return _device(x, y, z + h, c)

    def each(fn):
        fn(0, 1 - c)

        for k in range(1, 16):
            fn(k, 0)
            fn(k, 1)

    barrier = pltpu.get_barrier_semaphore()

    def greet(device):
        pl.semaphore_signal(barrier, inc=1, device_id=device, device_id_type=MESH)

    each(lambda k, core: greet(plane_peer(k, core)))
    for h in range(1, NZ):
        greet(_device(x, y, z + h, c))
    greeted = 31 + 7
    if TWIST:
        for dx, dy, dz in ((0, 0, 1), (1, 0, 1), (0, 1, 1), (0, 0, 2)):
            for sign in (1, -1):
                for core in (0, 1):
                    greet(_device(x + sign * dx, y + sign * dy, z + sign * dz, core))
                    greeted += 1
    pl.semaphore_wait(barrier, greeted)

    def send_j(k, core):
        s = colour((k >> 2), (k & 3), core)
        return pltpu.make_async_remote_copy(
            src_ref=j_ref.at[:, :, cols(s)], dst_ref=J1.at[d],
            send_sem=js, recv_sem=jr,
            device_id=plane_peer(k, core), device_id_type=MESH)

    def send_x(k, core):
        s = colour((k >> 2), (k & 3), core)
        return pltpu.make_async_remote_copy(
            src_ref=x_ref.at[:, cols(s)], dst_ref=X.at[2 * k + c],
            send_sem=xs, recv_sem=xr.at[k],
            device_id=peer(k, core), device_id_type=MESH)

    def send_a(k, core):
        return pltpu.make_async_remote_copy(
            src_ref=a_ref, dst_ref=A.at[2 * k + c],
            send_sem=as_, recv_sem=ar,
            device_id=peer(k, core), device_id_type=MESH)

    def all_of(buf, ssem, rsem, n=31):
        return pltpu.make_async_remote_copy(
            src_ref=buf.at[pl.ds(0, n)], dst_ref=buf.at[pl.ds(0, n)], send_sem=ssem, recv_sem=rsem,
            device_id=plane_peer(0, 1 - c), device_id_type=MESH)

    def send_s(k, core):
        return pltpu.make_async_remote_copy(
            src_ref=SS.at[2 * k + core], dst_ref=SR.at[2 * k + c],
            send_sem=ss, recv_sem=sr,
            device_id=peer(k, core, -1), device_id_type=MESH)

    def send_w(k, core):
        return pltpu.make_async_remote_copy(
            src_ref=WS, dst_ref=WB.at[2 * k + c],
            send_sem=ws, recv_sem=wr.at[k],
            device_id=peer(k, core), device_id_type=MESH)

    def send_g(h):
        q = SLOT[4 if h == 4 else -h]
        return pltpu.make_async_remote_copy(
            src_ref=PJ.at[0], dst_ref=PJ.at[q], send_sem=gs, recv_sem=gr.at[q],
            device_id=column_peer(h), device_id_type=MESH)

    def send_r(h):
        h = h % NZ
        return pltpu.make_async_remote_copy(
            src_ref=RS.at[h], dst_ref=RR.at[h], send_sem=rs, recv_sem=rr.at[h],
            device_id=column_peer(h), device_id_type=MESH)

    def send_f(k, core):
        q = (_mod(x + (k >> 2), NX) * NY + _mod(y + (k & 3), NY)) * 2 + core
        return pltpu.make_async_remote_copy(
            src_ref=FS.at[q], dst_ref=out_ref.at[:, :, cols(colour(0, 0, c))],
            send_sem=fs, recv_sem=fr,
            device_id=plane_peer(k, core), device_id_type=MESH)

    mine = colour(0, 0, c)
    own_x = pltpu.make_async_copy(x_ref.at[:, cols(mine)], X.at[c], lsem.at[0])
    own_j = pltpu.make_async_copy(j_ref.at[:, :, cols(mine)], J1.at[d], lsem.at[1])
    own_j.start()
    each(lambda k, core: send_j(k, core).start())
    own_x.start()

    def start_x(lo, hi):
        for k in range(lo, hi):
            send_x(k, 0).start()
            send_x(k, 1).start()

    send_x(0, 1 - c).start()
    start_x(1, EARLY)
    A[c] = a_ref[...]

    own_j.wait()
    all_of(J1, js, jr).wait_recv()
    for q in range(32):
        for kk in range(2):
            ASM[kk * 64 + 2 * q : kk * 64 + 2 * q + 2, :] = J1[q, kk].astype(F32)
    PJ[0] = ASM[...].astype(BF16)

    def halve(lo, hi):
        for q in range(lo, hi):
            v = PJ[q].astype(F32)
            H[q] = jnp.broadcast_to(0.5 * jnp.sum(v * v, axis=1, keepdims=True), (128, 128))

    for h in FAR_FIRST:
        send_g(h).start()
    each(lambda k, core: send_a(k, core).start())
    start_x(EARLY, 16)
    halve(0, 1)
    for h in FAR_FIRST:
        send_g(h).wait_recv()
        q = SLOT[4 if h == 4 else -h]
        halve(q, q + 1)

    own_x.wait()

    all_of(A, as_, ar).wait_recv()

    def choose(total, k, core, lo, hi):
        ids = jnp.broadcast_to(A[2 * k + core], (8, 128))
        for q in range(lo, hi):
            for kk in range(2):
                live = ids == 2 * ((z + PLANES[q]) & 7) + kk
                for g in range(8):
                    at = (q - lo) * 128 + kk * 64 + 8 * g
                    part = T[at : at + 8, core * 128 : (core + 1) * 128]
                    half = H[q, kk * 64 + 8 * g : kk * 64 + 8 * g + 8, :]
                    total[g] = jnp.where(live, part - half, total[g])
        return total

    def score(k, _):
        @pl.when(k == 0)
        def _():
            all_of(X, xs, xr.at[0], 1).wait_recv()

        @pl.when(k != 0)
        def _():
            all_of(X, xs, xr.at[k], 2).wait_recv()

        rows = X[pl.ds(2 * k, 2)].reshape(256, 256)
        T[...] = lax.dot_general(
            PJ[...].reshape(1024, 256), rows, (((1,), (1,)), ((), ())), preferred_element_type=F32)
        for core in range(2):
            total = choose([jnp.zeros((8, 128), F32)] * 8, k, core, 0, 8)
            for g in range(8):
                SS[2 * k + core, 8 * g : 8 * g + 8, :] = total[g]
        for core in range(2):
            @pl.when((k != 0) | (c != core))
            def _():
                send_s(k, core).start()
        return 0
    lax.fori_loop(0, 16, score, 0)

    all_of(SR, ss, sr).wait_recv()

    def gather(k, total):
        return total + SR[2 * k] + SR[2 * k + 1]
    total = lax.fori_loop(1, 16, gather, SS[c] + SR[1 - c])
    scores = total * s_ref[...].astype(F32)
    largest = jnp.max(scores, axis=0, keepdims=True)
    expo = jnp.exp(scores - largest)
    sums = jnp.sum(expo, axis=0, keepdims=True)
    weight = (expo / sums).astype(BF16)
    WS[...] = weight
    WB[c] = weight
    each(lambda k, core: send_w(k, core).start())
    ev_ref[...] = largest + jnp.log(sums)

    def accumulate(n, group, wait):
        for k in (2 * n, 2 * n + 1):
            if wait:
                @pl.when(k == 0)
                def _():
                    all_of(WB, ws, wr.at[0], 1).wait_recv()

                @pl.when(k != 0)
                def _():
                    all_of(WB, ws, wr.at[k], 2).wait_recv()
        for part in range(4):
            ids = jnp.broadcast_to(A[4 * n + part], (8, 128))
            w = WB[4 * n + part].astype(F32)
            for q in range(4):
                for kk in range(2):
                    at = q * 128 + kk * 64
                    live = ids == 2 * ((z + PLANES[4 * group + q]) & 7) + kk
                    for g in range(4):
                        pair = [jnp.where(live, w[16 * g + 8 * i : 16 * g + 8 * i + 8], 0.0) for i in range(2)]
                        WM[at + 16 * g : at + 16 * g + 16, part * 128 : (part + 1) * 128] = (
                            jnp.concatenate(pair, axis=0).astype(BF16))
        rows = X[pl.ds(4 * n, 4)].reshape(512, 256)
        ACC[group] += jnp.dot(WM[...], rows, preferred_element_type=F32)
        return 0

    ACC[...] = jnp.zeros_like(ACC)
    for group in (1, 0):
        lax.fori_loop(0, 8, lambda n, _, group=group: accumulate(n, group, group == 1), 0)
        for q in (3, 2, 1, 0):
            h = PLANES[4 * group + q]
            if h:
                RS[h % NZ] = ACC[group, q * 128 : (q + 1) * 128, :].astype(BF16)
                send_r(h).start()
    final = ACC[0, 0:128, :]
    for h in (-3, 3, -2, 2, 4, -1, 1):
        send_r(h).wait_recv()
        final = final + RR[h % NZ].astype(F32)
    ASM[...] = final
    for q in range(32):
        for kk in range(2):
            FS[q, kk] = ASM[kk * 64 + 2 * q : kk * 64 + 2 * q + 2, :]
    each(lambda k, core: send_f(k, core).start())
    out_ref[:, :, cols(mine)] = FS[d]
    all_of(FS, fs, fr).wait_recv()

    for buf, sem in ((J1, js), (A, as_), (X, xs), (SS, ss), (WB, ws), (FS, fs)):
        all_of(buf, sem, sem).wait_send()
    all_of(PJ, gs, gs, 7).wait_send()
    all_of(RS, rs, rs, 7).wait_send()


def deliver(sums_ref, evidence_ref, out_ref, ev_ref):
    out_ref[...] = sums_ref[...]
    ev_ref[...] = evidence_ref[...]


def on_device(particles, assign, inv_sigma, projections):
    dma = pltpu.SemaphoreType.DMA
    vmem = pltpu.VMEM
    sums, evidence = pl.pallas_call(
        kernel,
        name="estep",
        out_shape=(
            jax.ShapeDtypeStruct((2, 2, 8192), F32),
            jax.ShapeDtypeStruct((1, 128), F32),
        ),
        in_specs=[
            pl.BlockSpec(memory_space=pl.ANY),
            pl.BlockSpec(memory_space=pltpu.VMEM),
            pl.BlockSpec(memory_space=pltpu.VMEM),
            pl.BlockSpec(memory_space=pl.ANY),
        ],
        out_specs=(
            pl.BlockSpec(memory_space=pltpu.VMEM),
            pl.BlockSpec(memory_space=pltpu.VMEM),
        ),
        scratch_shapes=[
            vmem((32, 128, 256), BF16),
            vmem((32, 1, 128), jnp.int32),
            vmem((32, 2, 2, 256), BF16),
            vmem((128, 256), F32),
            vmem((8, 128, 256), BF16),
            vmem((8, 128, 128), F32),
            vmem((1024, 256), F32),
            vmem((32, 64, 128), F32),
            vmem((32, 64, 128), F32),
            vmem((64, 128), BF16),
            vmem((32, 64, 128), BF16),
            vmem((512, 512), BF16),
            vmem((2, 512, 256), F32),
            vmem((8, 128, 256), BF16),
            vmem((8, 128, 256), BF16),
            vmem((32, 2, 2, 256), F32),
            dma((2,)),
            dma, dma((16,)),
            dma, dma,
            dma, dma,
            dma, dma((8,)),
            dma, dma,
            dma, dma((16,)),
            dma, dma((8,)),
            dma, dma,
        ],
        compiler_params=pltpu.CompilerParams(collective_id=0, has_side_effects=True),
    )(particles, assign.reshape(1, 128), inv_sigma.reshape(1, 128), projections)
    sums, evidence = pl.pallas_call(
        deliver,
        name="deliver",
        out_shape=(
            jax.ShapeDtypeStruct((2, 2, 8192), F32),
            jax.ShapeDtypeStruct((1, 128), F32),
        ),
    )(sums, evidence)
    return sums, evidence.reshape(128)


def solution(mesh):
    return jax.shard_map(
        on_device,
        mesh=mesh,
        in_specs=(
            P(("cls", "dom"), None),
            P(("cls", "dom"), None),
            P(("cls", "dom")),
            P("cls", "dom", None),
        ),
        out_specs=(P("cls", "dom", None), P(("cls", "dom"))),
        check_vma=False,
    )
```
